32 devices in a mesh: frame: 8 (over z, core), space: 4 (over y, x).
Axes of the slice: x: 2, y: 2, z: 4, core: 2. Of those that a mesh axis runs over, the one named last changes fastest.
Arguments:
- spatial_query: bfloat16 [8, 256, 1152], P('frame', 'space'), may hold values from -24 to 24
- spatial_key: bfloat16 [8, 256, 1152], P('frame', 'space'), may hold values from -24 to 24
- spatial_value: bfloat16 [8, 256, 1152], P('frame', 'space'), may hold values from -6 to 6
- latents: bfloat16 [8, 256, 1152], P('frame', 'space'), may hold values from -6 to 6
- proj_weight: bfloat16 [1152, 1152], P('frame'), may hold values from -0.1875 to 0.1875
- proj_bias: float32 [1152], replicated, may hold values from -3 to 3
- residual_gate: float32 [1152], replicated, may hold values from 0.5 to 1.5
- temporal_shift: float32 [1152], replicated, may hold values from -3 to 3
- temporal_scale: float32 [1152], replicated, may hold values from -0.5 to 0.5
- temporal_weight: bfloat16 [1152, 3456], P('frame'), may hold values from -0.75 to 0.75
- clip_lengths: int32 [4], replicated, may hold values from 1 to 4, 8 in all
Outputs:
- hidden: float32 [8, 256, 1152], P('frame', 'space')
- temporal_out: float32 [8, 256, 1152], P('frame', 'space')
The draws below stay inside these ranges and needn't reach their ends.
Inputs may be any that keep to these rules, and one draw needn't show every extreme that they name: `clip_lengths`: 4 clips fill the 8 frames in order; one clip has exactly 4 frames.
All inputs are finite; a program needn't handle non-finite values.
Results may differ from the reference program's by a relative error of at most 0.012.
Values may be sent and summed in bfloat16 or wider, within the bound.
No kernel may reach another device: no remote copies, remote signals or barrier semaphores. Data moves between devices by JAX's collectives and lax.ppermute only.
A program may use at most 64 MiB of HBM per device.

```python
import math
import jax
import jax.numpy as jnp
import numpy as np
from jax import lax

D = 1152
HEADS = 16
FRAMES = 8
PATCHES = 256
CLIPS = 4
MOST = 4


def boosted_heads(key):
    base = jnp.clip(2.0 * jax.random.normal(key, (FRAMES, PATCHES, D), jnp.float32), -8.0, 8.0)
    return base


def draw_spatial_query(key, part):
    return boosted_heads(jax.random.fold_in(key, 11)).astype(jnp.bfloat16)


def draw_spatial_key(key, part):
    return boosted_heads(jax.random.fold_in(key, 12)).astype(jnp.bfloat16)


def draw_temporal_weight(key, part):
    base = jnp.clip(jax.random.normal(jax.random.fold_in(key, 13), (D, 3 * D), jnp.float32), -4.0, 4.0)
    return jnp.clip(base * (1.0 / math.sqrt(D)), -0.75, 0.75).astype(jnp.bfloat16)


def block_scale(rng, extent, cuts, smallest, largest):
    def one(dim, parts):
        steps = jax.random.uniform(jax.random.fold_in(jax.random.fold_in(rng, 6), dim), (parts,), jnp.float32, smallest / len(cuts), largest / len(cuts))
        return jnp.repeat(jnp.exp(steps), extent[dim] // parts).reshape((-1,) + (1,) * (len(extent) - dim - 1))

    level = one(*cuts[0])
    for cut in cuts[1:]:
        level = level * one(*cut)
    return level


def profile(amount, total, reach, lean):
    loads = [(1 << 20) // math.isqrt(standing ** lean) + 1 for standing in range(2, amount + 1)]
    rest, counts = total - reach - (amount - 1), [1] * (amount - 1)
    while rest > 0:
        free = [i for i in range(amount - 1) if counts[i] < reach]
        mass, left = sum([loads[i] for i in free]), rest
        for i in free:
            more = min(reach - counts[i], max(1, left * loads[i] // mass), rest)
            counts[i] = counts[i] + more
            rest = rest - more
    return np.array([reach] + counts)


def uneven(rng, count, total, reach, skew):
    if count == 2:
        one = jax.random.randint(rng, (), max(1, total - reach), min(reach, total - 1) + 1)
        return jnp.stack([one, total - one])
    tallies = jnp.asarray(profile(count, total, reach, skew), jnp.int32)
    pairs = (count - 1) // 2
    giver, sink = tallies[1:1 + 2 * pairs:2], tallies[2:2 + 2 * pairs:2]
    slack = jnp.minimum(giver - 1, reach - sink)
    passed = jax.random.randint(jax.random.fold_in(rng, 1), (pairs,), 0, 1 << 20) % (slack + 1)
    tallies = tallies.at[1:1 + 2 * pairs:2].set(giver - passed).at[2:2 + 2 * pairs:2].set(sink + passed)
    return tallies[jax.random.permutation(jax.random.fold_in(rng, 2), count)]


def bell_draw(own_key, dims, deviation, limit, shards=(), kind=jnp.bfloat16):
    values = jax.random.normal(own_key, dims, jnp.float32) * deviation
    if len(shards) > 0:
        values = block_scale(own_key, dims, shards, -0.22, 0.18) * values
    return jnp.clip(values, min=-limit, max=limit).astype(kind)


def setup_inputs(seed: int = 0) -> dict:
    splits = jax.random.split(jax.random.key(seed), 12)
    return {
        "spatial_query": draw_spatial_query(jax.random.fold_in(splits[11], 71), 0),
        "spatial_key": draw_spatial_key(jax.random.fold_in(splits[11], 71), 0),
        "spatial_value": bell_draw(splits[2], (FRAMES, PATCHES, D), 1.0, 6.0, ((0, 8), (1, 4))),
        "latents": bell_draw(splits[3], (FRAMES, PATCHES, D), 1.0, 6.0, ((0, 8), (1, 4))),
        "proj_weight": bell_draw(splits[4], (D, D), D ** -0.5, 0.1875, ((0, 8),)),
        "proj_bias": bell_draw(splits[5], (D,), 0.5, 3.0, (), jnp.float32),
        "residual_gate": jnp.clip(jax.random.uniform(splits[6], (D,), jnp.float32, 0.5, 1.5), 0.5, 1.5),
        "temporal_shift": bell_draw(splits[7], (D,), 0.5, 3.0, (), jnp.float32),
        "temporal_scale": jnp.clip(jax.random.uniform(splits[8], (D,), jnp.float32, -0.5, 0.5), -0.5, 0.5),
        "temporal_weight": draw_temporal_weight(jax.random.fold_in(splits[11], 71), 0),
        "clip_lengths": uneven(splits[10], CLIPS, FRAMES, MOST, 2).astype(jnp.int32),
    }


def attend(query, keys, values, allowed):
    scale = 1.0 / math.sqrt(query.shape[-1])
    scores = jnp.einsum('qhd,khd->hqk', query.astype(jnp.float32), keys.astype(jnp.float32)) * scale
    if allowed is not None:
        scores = jnp.where(allowed[None, :, :], scores, -1e+30)
    top = lax.optimization_barrier(jnp.max(scores, axis=-1, keepdims=True))
    probs = jnp.exp(scores - top)
    total = lax.optimization_barrier(jnp.sum(probs, axis=-1))
    weights = lax.optimization_barrier(probs.astype(jnp.bfloat16))
    mixed = jnp.einsum('hqk,khd->qhd', weights.astype(jnp.float32), values.astype(jnp.float32))
    return mixed / jnp.transpose(total)[:, :, None]

def reference(spatial_query, spatial_key, spatial_value, latents, proj_weight, proj_bias, residual_gate, temporal_shift, temporal_scale, temporal_weight, clip_lengths):
    head_dim = D // HEADS

    def one_frame(frame):
        fq, fk, fv = frame
        split = (PATCHES, HEADS, head_dim)
        return attend(fq.reshape(split), fk.reshape(split), fv.reshape(split), None).reshape(PATCHES, D).astype(jnp.bfloat16)
    attended = lax.map(one_frame, (spatial_query, spatial_key, spatial_value))
    flat = attended.reshape(FRAMES * PATCHES, D)
    projected = jnp.dot(flat, proj_weight, preferred_element_type=jnp.float32)
    hidden = latents.reshape(FRAMES * PATCHES, D).astype(jnp.float32) + residual_gate * (projected + proj_bias)
    mean = lax.optimization_barrier(jnp.mean(hidden, axis=-1, keepdims=True))
    centred = hidden - mean
    variance = lax.optimization_barrier(jnp.mean(centred * centred, axis=-1, keepdims=True))
    normed = (centred * lax.rsqrt(variance + 1e-06) * (1.0 + temporal_scale) + temporal_shift).astype(jnp.bfloat16)
    packed = jnp.dot(normed, temporal_weight, preferred_element_type=jnp.float32).astype(jnp.bfloat16)
    packed = jnp.transpose(packed.reshape(FRAMES, PATCHES, 3 * D), (1, 0, 2))
    ends = jnp.cumsum(clip_lengths.astype(jnp.int32))
    clip_of = lax.optimization_barrier(jnp.sum((jnp.arange(FRAMES, dtype=jnp.int32)[:, None] >= ends[None, :]).astype(jnp.int32), axis=1))
    allowed = clip_of[:, None] == clip_of[None, :]

    def one_position(rows):
        split = (FRAMES, HEADS, head_dim)
        query = rows[:, :D].reshape(split)
        keys = rows[:, D:2 * D].reshape(split)
        values = rows[:, 2 * D:].reshape(split)
        return attend(query, keys, values, allowed).reshape(FRAMES, D)
    temporal = lax.map(one_position, packed)
    temporal_out = jnp.transpose(temporal, (1, 0, 2))
    return (hidden.reshape(FRAMES, PATCHES, D), temporal_out)
```

```python
import math

import jax
import jax.numpy as jnp
from jax import lax
from jax.sharding import PartitionSpec as P

HEADS = 16
BOTH = ("frame", "space")

neg_fill = -1e30


def spatial_mix(query, keys, values):
    factor = 1.0 / math.sqrt(query.shape[-1])
    scores = jnp.einsum("ahd,bhd->hab", query, keys, preferred_element_type=jnp.float32) * factor
    top = jnp.max(scores, axis=-1, keepdims=True)
    probs = jnp.exp(scores - top)
    total = jnp.sum(probs, axis=-1)
    mixed = jnp.einsum(
        "hab,bhd->ahd", probs.astype(jnp.bfloat16), values, preferred_element_type=jnp.float32
    )
    return mixed / jnp.transpose(total)[..., None]


def temporal_mix(query, keys, values, allowed):
    factor = 1.0 / math.sqrt(query.shape[-1])
    scores = (
        jnp.einsum("sanhd,sbnhd->snhab", query, keys, preferred_element_type=jnp.float32) * factor
    )
    scores = jnp.where(allowed, scores, neg_fill)
    top = jnp.max(scores, axis=-1, keepdims=True)
    probs = jnp.exp(scores - top)
    total = jnp.sum(probs, axis=-1)
    mixed = jnp.einsum(
        "snhab,sbnhd->sanhd", probs.astype(jnp.bfloat16), values, preferred_element_type=jnp.float32
    )
    return mixed / jnp.transpose(total, (0, 3, 1, 2))[..., None]


def swap_pairs(x):
    size = lax.axis_size("frame")
    return lax.ppermute(x, "frame", [(i, i ^ 1) for i in range(size)])


def proj_rows(proj_weight):
    groups, spaces = lax.axis_size("frame"), lax.axis_size("space")
    if groups != 2 * spaces:
        whole = lax.all_gather(proj_weight, "frame", axis=0, tiled=True)
        count = whole.shape[0] // spaces
        return lax.dynamic_slice_in_dim(whole, lax.axis_index("space") * count, count, 0)
    perm = [
        ((2 * s + j) * spaces + t, (2 * t + j) * spaces + s)
        for s in range(spaces)
        for t in range(spaces)
        for j in range(2)
    ]
    mine = lax.ppermute(proj_weight, BOTH, perm)
    other = swap_pairs(mine)
    even = lax.axis_index("frame") % 2 == 0
    return jnp.concatenate([jnp.where(even, mine, other), jnp.where(even, other, mine)], axis=0)


def head_columns(temporal_weight):
    groups, spaces = lax.axis_size("frame"), lax.axis_size("space")
    rows, cols = temporal_weight.shape
    width = cols // 3
    take = width // spaces
    start = lax.axis_index("space") * take
    parts = [
        lax.dynamic_slice_in_dim(temporal_weight, i * width + start, take, 1) for i in range(3)
    ]
    heads = HEADS // spaces
    if groups % 2 or heads % 2:
        piece = jnp.concatenate(parts, axis=1)
        return [lax.all_gather(piece, "frame", axis=0, tiled=True)]
    half = take // 2
    halves = [jnp.concatenate([p[:, h * half : (h + 1) * half] for p in parts], axis=1) for h in range(2)]
    send = jnp.stack([halves[f % 2] for f in range(groups)])
    mine = lax.all_to_all(send, "frame", split_axis=0, concat_axis=0, tiled=True)
    mine = mine.reshape(groups * rows, 3 * half)
    return [mine, swap_pairs(mine)]


def shards(
    spatial_query,
    spatial_key,
    spatial_value,
    latents,
    proj_weight,
    proj_bias,
    residual_gate,
    temporal_shift,
    temporal_scale,
    temporal_weight,
    clip_lengths,
):
    frames_dev, count, width = latents.shape
    assert frames_dev == 1
    groups, spaces = lax.axis_size("frame"), lax.axis_size("space")
    heads = HEADS // spaces
    head_dim = width // HEADS
    take = heads * head_dim
    per_group = count // groups

    parts = [x.reshape(count, spaces, take) for x in (spatial_query, spatial_key, spatial_value)]
    sent = jnp.transpose(jnp.concatenate(parts, axis=-1), (1, 0, 2))
    got = lax.all_to_all(sent, "space", split_axis=0, concat_axis=0, tiled=True)
    got = got.reshape(spaces * count, 3, heads, head_dim)
    attended = spatial_mix(got[:, 0], got[:, 1], got[:, 2]).astype(jnp.bfloat16)
    partial = jnp.dot(
        attended.reshape(spaces * count, take),
        proj_rows(proj_weight),
        preferred_element_type=jnp.float32,
    ).astype(jnp.bfloat16)
    partial = lax.all_to_all(
        partial.reshape(spaces, count, width), "space", split_axis=0, concat_axis=0, tiled=True
    )
    projected = jnp.sum(partial.astype(jnp.float32), axis=0)
    hidden = latents.reshape(count, width).astype(jnp.float32) + residual_gate * (
        projected + proj_bias
    )
    mean = jnp.mean(hidden, axis=-1, keepdims=True)
    centred = hidden - mean
    variance = jnp.mean(centred * centred, axis=-1, keepdims=True)
    normed = (
        centred * lax.rsqrt(variance + 1e-06) * (1.0 + temporal_scale) + temporal_shift
    ).astype(jnp.bfloat16)

    tokens = lax.all_to_all(
        normed.reshape(groups, per_group, width), "frame", split_axis=0, concat_axis=0, tiled=True
    )
    tokens = lax.all_gather(tokens, "space", axis=0)

    ends = jnp.cumsum(clip_lengths)
    clip_of = jnp.sum(
        (jnp.arange(groups, dtype=jnp.int32)[:, None] >= ends[None, :]).astype(jnp.int32), axis=1
    )
    allowed = clip_of[:, None] == clip_of[None, :]
    pieces = head_columns(temporal_weight)
    mixed = []
    for piece in pieces:
        packed = jnp.einsum(
            "sfnc,ce->sfne", tokens, piece, preferred_element_type=jnp.float32
        ).astype(jnp.bfloat16)
        packed = packed.reshape(spaces, groups, per_group, 3, heads // len(pieces), head_dim)
        mixed.append(
            temporal_mix(packed[:, :, :, 0], packed[:, :, :, 1], packed[:, :, :, 2], allowed)
        )
    mixed = jnp.concatenate(mixed, axis=3).astype(jnp.bfloat16)
    mixed = mixed.reshape(spaces, groups, per_group, take)
    back = jnp.transpose(mixed, (1, 0, 2, 3)).reshape(groups * spaces, per_group, take)
    back = lax.all_to_all(back, BOTH, split_axis=0, concat_axis=0, tiled=True)
    back = back.reshape(groups, spaces, per_group, len(pieces), take // len(pieces))
    if len(pieces) == 2:
        back = jnp.stack([b if f % 2 == 0 else b[:, :, ::-1] for f, b in enumerate(back)])
    temporal_out = jnp.transpose(back.reshape(groups, spaces, per_group, take), (0, 2, 1, 3))
    temporal_out = temporal_out.reshape(1, count, width).astype(jnp.float32)
    return (hidden.reshape(1, count, width), temporal_out)


def solution(mesh):
    in_specs = (
        P("frame", "space", None),
        P("frame", "space", None),
        P("frame", "space", None),
        P("frame", "space", None),
        P("frame", None),
        P(),
        P(),
        P(),
        P(),
        P("frame", None),
        P(),
    )
    out_specs = (P("frame", "space", None), P("frame", "space", None))
    return jax.shard_map(shards, mesh=mesh, in_specs=in_specs, out_specs=out_specs, check_vma=False)
```
